32 devices in a mesh: groups: 2 (over x), row: 16 (over z, y, core).
Axes of the slice: x: 2, y: 2, z: 4, core: 2. Of those that a mesh axis runs over, the one named last changes fastest.
Arguments:
- fit_first: bfloat16 [128, 512, 1536], P('groups', 'row'), parts along dimension 0, may hold values from -1 to 1
- fit_second: bfloat16 [4, 512, 1536], P('groups', 'row'), parts along dimension 0, may hold values from -1 to 1
- amplitudes: bfloat16 [1024, 512, 512], P('groups', None, 'row'), parts along dimension 0, may hold values from -0.015625 to 0.015625
Outputs:
- ladder: float32 [128, 2, 512], P('groups', None, 'row'), parts along dimension 0
The draws below stay inside these ranges and needn't reach their ends.
There are 2 independent parts, one for each index of `groups`. The reference program is written for one: setup_inputs(seed, part) draws one part's arguments, and reference() takes and returns one part's arrays. A program takes and returns all parts, laid end to end along the dimension named above; each array names one. Nothing has to cross between parts.
All inputs are finite; a program needn't handle non-finite values.
Results may differ from the reference program's by a relative error of at most 0.0029.
Values may be sent and summed in bfloat16 or wider, within the bound.
No kernel may reach another device: no remote copies, remote signals or barrier semaphores. Data moves between devices by JAX's collectives and lax.ppermute only.
A program may use at most 128 MiB of HBM per device.

```python
import jax
import jax.numpy as jnp
from jax import lax

V = 512
Q = 1536
PAIRS = 512
WB = 2
A = 64


def with_spikes(drawn, rng, source, target, parts, factor):
    owner, partner = [(jnp.arange(drawn.shape[dim]) // (drawn.shape[dim] // parts)).reshape([-1 if axis == dim else 1 for axis in range(drawn.ndim)]) for dim in (source, target)]
    chosen = jax.random.permutation(rng, parts)[partner]
    strong = (owner == chosen) | (owner == (partner + parts // 2) % parts)
    return jnp.where(strong, factor * drawn, drawn)


def levels(rng, dims, shards, smallest, largest):
    def one(axis_at, blocks):
        draws = jax.random.uniform(jax.random.fold_in(jax.random.fold_in(rng, 6), axis_at), (blocks,), jnp.float32, smallest / len(shards), largest / len(shards))
        return jnp.repeat(jnp.exp(draws), dims[axis_at] // blocks).reshape((-1,) + (1,) * (len(dims) - axis_at - 1))

    gain = one(*shards[0])
    for cut in shards[1:]:
        gain = gain * one(*cut)
    return gain


def centred(stream_key, extent, scale, bound, cuts=(), kind=jnp.bfloat16):
    loudness = levels(stream_key, extent, cuts, -0.22, 0.18) if cuts else 1.0
    array = jax.random.normal(stream_key, extent, jnp.float32) * scale * loudness
    return jnp.minimum(jnp.maximum(array, -bound), bound).astype(kind)


def heavy_noise(rng, dims, deviation, reach, split, heavy, kind=jnp.bfloat16):
    entries = deviation * jax.random.normal(rng, dims, jnp.float32)
    if split:
        entries = entries * levels(rng, dims, split, -0.22, 0.18)
    return jnp.clip(with_spikes(entries, jax.random.fold_in(rng, 3), *heavy), -reach, reach).astype(kind)


def setup_inputs(seed: int = 0, part: int = 0) -> dict:
    arg_keys = jax.random.split(jax.random.key(seed), 4)
    part_keys = jax.random.split(jax.random.fold_in(arg_keys[3], part), 4)
    fit_first = centred(part_keys[0], (A, V, Q), 0.16, 1.0, ((1, 16),))
    fit_second = centred(part_keys[1], (WB, V, Q), 0.16, 1.0, ((1, 16),))
    amplitudes = heavy_noise(part_keys[2], (V, V, PAIRS), (V * V) ** -0.5, 0.015625, ((2, 16),), (0, 2, 16, 2.0))
    return dict(fit_first=fit_first, fit_second=fit_second, amplitudes=amplitudes)


def reference(fit_first, fit_second, amplitudes):
    width_v = fit_first.shape[1]
    width_b = fit_second.shape[0]
    right_rows = fit_second.reshape(width_b * width_v, fit_second.shape[2])
    amp_full = amplitudes.astype(jnp.float32)

    def one_index(first_row):
        integrals = jnp.dot(first_row, right_rows.T, preferred_element_type=jnp.float32).astype(jnp.bfloat16)
        integrals = integrals.reshape(width_v, width_b, width_v).astype(jnp.float32)
        return jnp.einsum("cbd,cdp->bp", integrals, amp_full, precision=lax.Precision.HIGHEST)

    return lax.map(one_index, fit_first)
```

```python
from functools import partial

import jax
import jax.numpy as jnp
from jax import lax
from jax.experimental import pallas as pl
from jax.experimental.pallas import tpu as pltpu
from jax.sharding import PartitionSpec as P

PLANES = 4
MEMBERS = 4


def general_shards(fit_first, fit_second, amplitudes):
    first_count, block_count, factors = fit_first.shape
    left_rows = fit_first.reshape(first_count * block_count, factors)
    every_factor = lax.all_gather(fit_second, "row", axis=1, tiled=True)
    width_b, depth, _ = every_factor.shape
    right_rows = every_factor.reshape(width_b * depth, factors)
    integrals = lax.dot_general(
        left_rows, right_rows, (((1,), (1,)), ((), ())), preferred_element_type=jnp.float32
    ).astype(jnp.bfloat16)
    integrals = integrals.reshape(first_count, block_count, width_b, depth)
    local_amps = lax.all_to_all(amplitudes, "row", split_axis=0, concat_axis=2, tiled=True)
    partial_value = jnp.einsum(
        "acbd,cdp->abp", integrals, local_amps, preferred_element_type=jnp.float32
    )
    return lax.psum_scatter(partial_value, "row", scatter_dimension=2, tiled=True)


def nt(left, right):
    return lax.dot_general(left, right, (((1,), (1,)), ((), ())), preferred_element_type=jnp.float32)


def integrals_body(left_ref, right_ref, out_ref):
    out_ref[...] = nt(left_ref[...], right_ref[...]).astype(out_ref.dtype)


def integrals_chunk(left_rows, right_rows, row_block):
    rows, factors = left_rows.shape
    cols = right_rows.shape[0]
    return pl.pallas_call(
        integrals_body,
        grid=(rows // row_block,),
        in_specs=[
            pl.BlockSpec((row_block, factors), lambda i: (i, 0)),
            pl.BlockSpec((cols, factors), lambda i: (0, 0)),
        ],
        out_specs=pl.BlockSpec((row_block, cols), lambda i: (i, 0)),
        out_shape=jax.ShapeDtypeStruct((rows, cols), jnp.bfloat16),
        cost_estimate=pl.CostEstimate(
            flops=2 * rows * cols * factors, transcendentals=0,
            bytes_accessed=2 * (rows * factors + cols * factors + rows * cols)),
        name="integrals_chunk",
    )(left_rows, right_rows)


def contract_body(counts, slots_ref, *refs):
    n_ints, n_alt, n_amps, n_amps_alt, step, width = counts
    ints = refs[:n_ints]
    ints_alt = refs[n_ints:n_ints + n_alt]
    refs = refs[n_ints + n_alt:]
    amps = refs[:n_amps]
    amps_alt = refs[n_amps:n_amps + n_amps_alt]
    acc_ref, out_ref = refs[n_amps + n_amps_alt:]

    @pl.when(pl.program_id(0) == 0)
    def _():
        out_ref[...] = acc_ref[...]

    total = out_ref[...]
    for at in range(step):
        for j in range(n_ints):
            here = pl.ds(pl.multiple_of(slots_ref[j] * width, width), width)
            block = ints[j][at]
            if ints_alt:
                block = block + ints_alt[j][at]
            right = jnp.concatenate([block[:, :width], block[:, width:]], axis=0)
            pieces = [ref[at, :, here] for ref in amps]
            half = n_amps - n_amps_alt
            for i, ref in enumerate(amps_alt):
                pieces[half + i] = pieces[half + i] + ref[at, :, here]
            total = total + nt(jnp.concatenate(pieces, axis=0), right)
    out_ref[...] = total


def contract(slots, ints, ints_alt, amps, amps_alt, acc, step, width):
    count = ints[0].shape[0]
    int_spec = pl.BlockSpec((step,) + ints[0].shape[1:], lambda i, s: (i, 0, 0))
    amp_spec = pl.BlockSpec((step,) + amps[0].shape[1:], lambda i, s: (i, 0, 0))
    acc_spec = pl.BlockSpec(acc.shape, lambda i, s: (0, 0))
    counts = (len(ints), len(ints_alt), len(amps), len(amps_alt), step, width)
    flops = 2 * acc.shape[0] * acc.shape[1] * count * width * len(ints)
    moved = sum(2 * x.size for x in (*ints, *ints_alt, *amps, *amps_alt))
    return pl.pallas_call(
        partial(contract_body, counts),
        grid_spec=pltpu.PrefetchScalarGridSpec(
            num_scalar_prefetch=1,
            grid=(count // step,),
            in_specs=[int_spec] * (len(ints) + len(ints_alt))
            + [amp_spec] * (len(amps) + len(amps_alt)) + [acc_spec],
            out_specs=acc_spec,
        ),
        out_shape=jax.ShapeDtypeStruct(acc.shape, jnp.float32),
        cost_estimate=pl.CostEstimate(flops=flops, transcendentals=0, bytes_accessed=moved),
        name="contract",
    )(slots, *ints, *ints_alt, *amps, *amps_alt, acc)


def line_shards(fit_first, fit_second, amplitudes):
    first_count, block_c, factors = fit_first.shape
    width_b, block_d, _ = fit_second.shape
    pairs = amplitudes.shape[2]
    me = lax.axis_index("row")
    plane, member = me // MEMBERS, me % MEMBERS

    def send(value, move):
        table = []
        for z in range(PLANES):
            for w in range(MEMBERS):
                to = move(z, w)
                if to is not None and 0 <= to[0] < PLANES:
                    table.append((z * MEMBERS + w, to[0] * MEMBERS + to[1]))
        return lax.ppermute(value, "row", table)

    def across(value, mask):
        return value if mask == 0 else send(value, lambda z, w: (z, w ^ mask))

    def along(value, shift, only=None):
        return send(value, lambda z, w: (z + shift, w) if only is None or z in only else None)

    mine = [fit_second]
    for shift in range(1, PLANES):
        mine.append(send(fit_second, lambda z, w, shift=shift: ((z + shift) % PLANES, w)))

    def of_plane(pieces):
        every = jnp.zeros((width_b, MEMBERS * block_d, factors), fit_second.dtype)
        for mask, piece in enumerate(pieces):
            every = lax.dynamic_update_slice_in_dim(every, piece, (member ^ mask) * block_d, axis=1)
        return every.reshape(width_b * MEMBERS * block_d, factors)

    first = of_plane([across(fit_second, m) for m in range(MEMBERS)])
    rest = jnp.stack(mine[1:])
    rest_y = across(rest, 2)
    both = jnp.stack([rest, rest_y])
    both_k = across(both, 1)
    factors_of = [first] + [
        of_plane([both[0, j], both_k[0, j], both[1, j], both_k[1, j]]) for j in range(PLANES - 1)
    ]

    rows = jnp.transpose(amplitudes, (0, 2, 1))

    def piece_of(delta, mask):
        block = ((plane + delta) % PLANES) * MEMBERS + (member ^ mask)
        return lax.dynamic_slice_in_dim(rows, block * block_c, block_c, axis=0)

    amps = {delta: [across(piece_of(delta, m), m) for m in range(MEMBERS)] for delta in (-1, 1, 0, 2)}
    extra_up = [along(x, 1, only=(0,)) for x in amps[-1]]
    extra_down = [along(x, -1, only=(PLANES - 1,)) for x in amps[1]]

    left_rows = jnp.transpose(fit_first, (1, 0, 2)).reshape(block_c * first_count, factors)
    width = MEMBERS * block_d
    own, up, down, up2, down2 = [], [], [], [], []
    for j in range(PLANES):
        chunk = integrals_chunk(left_rows, factors_of[j], min(512, left_rows.shape[0]))
        chunk = chunk.reshape(block_c, first_count, width_b * width)
        own.append(chunk)
        up.append(along(chunk, 1))
        down.append(along(chunk, -1))
    for j in range(PLANES):
        up2.append(along(up[j], 1, only=(1, 2)))
        down2.append(along(down[j], -1, only=(1, 2)))

    steps = jnp.arange(PLANES, dtype=jnp.int32)

    def slots(delta):
        return (plane + delta - steps) % PLANES

    acc = jnp.zeros((MEMBERS * pairs, width_b * first_count), jnp.float32)
    acc = contract(slots(0), own, [], amps[0], [], acc, 8, width)
    acc = contract(slots(-1), up, [], amps[-1], [], acc, 8, width)
    acc = contract(slots(1), down, [], amps[1], [], acc, 8, width)
    both_acc = jnp.concatenate([acc, jnp.zeros_like(acc)], axis=0)
    for j in range(PLANES):
        both_acc = contract(
            slots(2)[j:j + 1], [up2[j]], [down2[j]], amps[2] + extra_up, extra_down, both_acc, 8, width)
    pieces = both_acc.reshape(2 * MEMBERS, pairs, width_b * first_count)
    total = pieces[0]
    for mask in range(1, MEMBERS):
        total = total + across(pieces[mask], mask)
    for mask in range(MEMBERS):
        total = total + send(
            pieces[MEMBERS + mask], lambda z, w, mask=mask: ({1: 0, PLANES - 2: PLANES - 1}.get(z, -1), w ^ mask))
    out = total.reshape(pairs, width_b, first_count)
    return jnp.transpose(out, (2, 1, 0))


def solution(mesh):
    placed = (P("groups", "row", None), P("groups", "row", None), P("groups", None, "row"))

    def shards(fit_first, fit_second, amplitudes):
        in_line = mesh.shape["row"] == PLANES * MEMBERS and fit_second.shape[0] == 2
        body = line_shards if in_line else general_shards
        return body(fit_first, fit_second, amplitudes)

    return jax.shard_map(
        shards, mesh=mesh, in_specs=placed, out_specs=P("groups", None, "row"), check_vma=False
    )
```
